32 devices in a mesh: pair: 4 (over y, x), tile: 8 (over z, core).
Axes of the slice: x: 2, y: 2, z: 4, core: 2. Of those that a mesh axis runs over, the one named last changes fastest.
Arguments:
- residual: float32 [24, 32, 64, 128], P('pair', 'tile'), parts along dimension 0, may hold values from -8 to 8
- coupling: float32 [32, 256, 128], P('tile', 'pair'), parts along dimension 1, may hold values from 0.1 to 4
- owners: int32 [8, 16], P('tile'), may hold values from 0 to 7
- earth: int32 [8, 16], P('tile'), may hold values 0 or 1
- sweep_counts: int32 [8], P('tile'), may hold values from 2 to 8, as said below
- coarse_inverse: float32 [768, 192], P('pair'), parts along dimension 0, may hold values from -2 to 2
- coarse_scale: float32 [8, 768], P('tile', 'pair'), parts along dimension 1, may hold values from 0.5 to 2
Outputs:
- preconditioned: float32 [24, 32, 64, 128], P('pair', 'tile'), parts along dimension 0
- image: float32 [24, 32, 64, 128], P('pair', 'tile'), parts along dimension 0
The draws below stay inside these ranges and needn't reach their ends.
There are 4 independent parts, one for each index of `pair`. The reference program is written for one: setup_inputs(seed, part) draws one part's arguments, and reference() takes and returns one part's arrays. A program takes and returns all parts, laid end to end along the dimension named above; an argument that names none is the same for every part. Nothing has to cross between parts.
Inputs may be any that keep to these rules, and one draw needn't show every extreme that they name: `owners`: each coarse block's owner is a tile. `sweep_counts`: some tile takes 8 sweeps.
All inputs are finite; a program needn't handle non-finite values. No bound on the sum of `earth` on one device may be relied on, other than what follows from the above.
Results may differ from the reference program's by a relative error of at most 0.0003.
Values sent between devices are 32-bit elements; how exact they have to be, the bound alone decides.
A program may use at most 64 MiB of HBM per device.

```python
import math
import jax
import jax.numpy as jnp
import numpy as np
from jax import lax

CX = 4
NY = 64
NZ = 128
MARGIN = 2
SWEEPS = 8
TILES = 8
NX = 32
NB = 16
BW = 192


def draw_residual(key, part):
    shape = (6, NX, NY, NZ)
    values = jnp.clip(jax.random.normal(key, shape, jnp.float32), -6.0, 6.0)
    return values


def draw_sweep_counts(key, part):
    key_counts = jax.random.fold_in(key, 11)
    key_index = jax.random.fold_in(key, 12)
    counts = jax.random.randint(key_counts, (TILES,), 2, SWEEPS + 1)
    chosen = jax.random.randint(key_index, (), 0, TILES)
    places = jnp.arange(TILES, dtype=jnp.int32)
    return jnp.where(places == chosen, SWEEPS, counts).astype(jnp.int32)


def draw_coarse_inverse(key, part):
    key_diag = jax.random.fold_in(key, 21)
    key_off = jax.random.fold_in(key, 22)
    rows = jnp.arange(BW, dtype=jnp.int32)
    unit = (rows[:, None] == rows[None, :]).astype(jnp.float32)
    diag = jax.random.uniform(key_diag, (BW, BW), jnp.float32, 1.0, 2.0)
    off = 0.03 * jnp.clip(jax.random.normal(key_off, (BW, BW), jnp.float32), -5.0, 5.0)
    return unit * diag + (1.0 - unit) * off


def plant(entries, rng, smallest, high):
    shape = entries.shape
    index_at = [jax.random.randint(jax.random.fold_in(rng, axis), (), 0, shape[axis]) for axis in range(len(shape))]
    entries = entries.at[tuple(index_at)].set(smallest)
    longest = shape.index(max(shape))
    index_at[longest] = (index_at[longest] + 1) % shape[longest]
    return entries.at[tuple(index_at)].set(high)


def block_scale(stream_key, shape, split, smallest, largest):
    level, own = 1.0, jax.random.fold_in(stream_key, 6)
    for dim, parts in split:
        heights = jnp.exp(jax.random.uniform(jax.random.fold_in(own, dim), (parts,), jnp.float32, smallest / len(split), largest / len(split)))
        level = level * jnp.repeat(heights, shape[dim] // parts).reshape([-1 if axis == dim else 1 for axis in range(len(shape))])
    return level


def rank_table(number_of, lean):
    loads = [(1 << 20) // math.isqrt(grade ** lean) + 1 for grade in range(1, number_of + 1)]
    spread = 1 + sum(loads) // (1 << 30)
    return np.cumsum(np.array([max(1, weight // spread) for weight in loads]))


def ranked_ids(own_key, shape, number_of, skew):
    grid = rank_table(number_of, skew)
    pick = jax.random.randint(jax.random.fold_in(own_key, 1), shape, 0, int(grid[number_of - 1]))
    rank = jnp.searchsorted(jnp.asarray(grid, jnp.int32), pick, side="right")
    return jax.random.permutation(jax.random.fold_in(own_key, 2), number_of)[rank].astype(jnp.int32)


def setup_inputs(seed: int = 0, part: int = 0) -> dict:
    key_list = jax.random.split(jax.random.key(seed), 8)
    own_keys = jax.random.split(jax.random.fold_in(key_list[7], part), 8)
    residual = draw_residual(jax.random.fold_in(jax.random.fold_in(key_list[7], part), 71), part)
    coupling = jnp.clip(jnp.exp(math.log(4.0) - 3.6888794 * jax.random.uniform(own_keys[1], (NX, NY, NZ), jnp.float32) ** block_scale(own_keys[1], (NX, NY, NZ), ((0, 8),), -0.2, 0.2)), 0.1, 4.0)
    owners = plant(ranked_ids(key_list[2], (TILES, NB), TILES, 1), jax.random.fold_in(key_list[2], 3), 0, TILES - 1).astype(jnp.int32)
    earth = plant((jax.random.randint(key_list[3], (TILES, NB), 0, 4) < 3).astype(jnp.int32), jax.random.fold_in(key_list[3], 1), 0, 1)
    sweep_counts = draw_sweep_counts(jax.random.fold_in(key_list[7], 71), part)
    coarse_inverse = draw_coarse_inverse(jax.random.fold_in(jax.random.fold_in(key_list[7], part), 71), part)
    coarse_scale = jnp.clip(jnp.exp(math.log(2.0) - 1.3862944 * jax.random.uniform(own_keys[6], (TILES, BW), jnp.float32) ** block_scale(own_keys[6], (TILES, BW), ((0, 8),), -0.2, 0.2)), 0.5, 2.0)
    return {"residual": residual, "coupling": coupling, "owners": owners, "earth": earth, "sweep_counts": sweep_counts, "coarse_inverse": coarse_inverse, "coarse_scale": coarse_scale}


damping = 0.4


def diff_next(values, along):
    length = values.shape[along]
    ahead = jnp.concatenate([lax.slice_in_dim(values, 1, length, axis=along), jnp.zeros_like(lax.slice_in_dim(values, 0, 1, axis=along))], axis=along)
    return ahead - values


def diff_prev(values, along):
    length = values.shape[along]
    behind = jnp.concatenate([jnp.zeros_like(lax.slice_in_dim(values, 0, 1, axis=along)), lax.slice_in_dim(values, 0, length - 1, axis=along)], axis=along)
    return values - behind


def scale_first(values, leading):
    return jnp.concatenate([values[:1] * leading, values[1:]], axis=0)


def curl_curl(field, leading):
    comp_x, comp_y, comp_z = field[0], field[1], field[2]
    face_x = scale_first(diff_next(comp_z, 1) - diff_next(comp_y, 2), leading)
    face_y = scale_first(diff_next(comp_x, 2) - diff_next(comp_z, 0), leading)
    face_z = scale_first(diff_next(comp_y, 0) - diff_next(comp_x, 1), leading)
    edge_x = diff_prev(face_z, 1) - diff_prev(face_y, 2)
    edge_y = diff_prev(face_x, 2) - diff_prev(face_z, 0)
    edge_z = diff_prev(face_y, 0) - diff_prev(face_x, 1)
    return jnp.stack([edge_x, edge_y, edge_z])


def operator(field, coupling, leading):
    real_part = field[:3]
    imag_part = field[3:]
    return jnp.concatenate([curl_curl(real_part, leading) - coupling * imag_part, curl_curl(imag_part, leading) + coupling * real_part], axis=0)


def sweep_once(iterate, rhs, coupling):
    denom = 1.0 / (16.0 + coupling * coupling)
    inverse_real = 4.0 * denom
    inverse_imag = -coupling * denom
    defect = rhs - operator(iterate, coupling, 1.0)
    def_real = defect[:3]
    def_imag = defect[3:]
    update = jnp.concatenate([inverse_real * def_real - inverse_imag * def_imag, inverse_real * def_imag + inverse_imag * def_real], axis=0)
    return iterate + damping * update


def reference(residual, coupling, owners, earth, sweep_counts, coarse_inverse, coarse_scale):
    width_ext = CX + 2 * MARGIN
    res_pad = jnp.pad(residual, ((0, 0), (MARGIN, MARGIN), (0, 0), (0, 0)))
    coup_pad = jnp.pad(coupling, ((MARGIN, MARGIN), (0, 0), (0, 0)))

    def one_tile(which):
        offset = (which * CX).astype(jnp.int32)
        rhs = lax.dynamic_slice_in_dim(res_pad, offset, width_ext, axis=1)
        coup = lax.dynamic_slice_in_dim(coup_pad, offset, width_ext, axis=0)
        sweeps = sweep_counts[which]

        def step_fn(step, iterate):
            return jnp.where(step < sweeps, sweep_once(iterate, rhs, coup), iterate)

        iterate = lax.fori_loop(0, SWEEPS, step_fn, jnp.zeros_like(rhs))
        return iterate[:, MARGIN:MARGIN + CX]

    local_part = lax.map(one_tile, jnp.arange(TILES, dtype=jnp.int32))
    local_part = jnp.transpose(local_part, (1, 0, 2, 3, 4)).reshape(6, NX, NY, NZ)
    coarse = residual.reshape(6, TILES, CX, NY // 4, 4, NZ // 4, 4).sum(axis=(2, 4, 6)) * (1.0 / 64.0)
    blocks = coarse.reshape(6, TILES, NY // 8, 2, NZ // 64, 16).transpose(1, 2, 4, 0, 3, 5).reshape(TILES, NB, BW)
    select = (owners[:, :, None] == jnp.arange(TILES, dtype=jnp.int32)[None, None, :]).astype(jnp.float32) * earth[:, :, None].astype(jnp.float32)
    aggregated = jnp.einsum('tbo,tbw->ow', select, blocks, precision=lax.Precision.HIGHEST)
    corrections = jnp.dot(aggregated, coarse_inverse.T, precision=lax.Precision.HIGHEST) * coarse_scale
    block_corr = jnp.einsum('tbo,ow->tbw', select, corrections, precision=lax.Precision.HIGHEST)
    fine = block_corr.reshape(TILES, NY // 8, NZ // 64, 6, 2, 16).transpose(3, 0, 1, 4, 2, 5).reshape(6, TILES, 1, NY // 4, 1, NZ // 4, 1)
    fine = jnp.broadcast_to(fine, (6, TILES, CX, NY // 4, 4, NZ // 4, 4)).reshape(6, NX, NY, NZ)
    preconditioned = local_part + fine
    image = operator(preconditioned, coupling, 1.0)
    return preconditioned, image
```

```python
import functools

import jax
import jax.numpy as jnp
from jax import lax
from jax.experimental import pallas as pl
from jax.experimental.pallas import tpu as pltpu
from jax.sharding import PartitionSpec as P

MARGIN = 2
SWEEPS = 8
damping = 0.4
HIGH = lax.Precision.HIGHEST
F32 = jnp.float32
SPLIT = ((1, 3), (4, 6))


def iota(shape, dim):
    return lax.broadcasted_iota(jnp.int32, shape, dim)


def z_next(x):
    width = x.shape[1]
    return jnp.where(iota(x.shape, 1) < width - 1, pltpu.roll(x, width - 1, 1), 0.0)


def z_prev(x):
    return jnp.where(iota(x.shape, 1) > 0, pltpu.roll(x, 1, 1), 0.0)


def y_next(x):
    edge = x[:8]
    edge = jnp.where(iota(edge.shape, 0) < 7, pltpu.roll(edge, 7, 0), 0.0)
    return jnp.concatenate([x[8:], edge], axis=0)


def y_prev(x):
    rows = x.shape[0]
    edge = x[rows - 8 :]
    edge = jnp.where(iota(edge.shape, 0) > 0, pltpu.roll(edge, 1, 0), 0.0)
    return jnp.concatenate([edge, x[: rows - 8]], axis=0)


def kernel(
    tiles,
    res, coup, owners, earth, sweeps, inv, scale,
    pre, img,
    rn, cn, rhs, coef, xs, hs, ys, gs, gx, hl, fine, pn, qn, w_ref, outbox, inbox, cbox, csrc,
    loc_sem, halo_send, halo_recv, s1, r1, s2, r2, fs, fr, out_sem,
):
    me = lax.axis_index("tile")
    planes = res.shape[1]
    ny, nz = res.shape[2], res.shape[3]
    groups = ny // 8
    ext = planes + 2 * MARGIN
    zblocks = nz // 64
    last = tiles - 1

    barrier = pltpu.get_barrier_semaphore()

    def greet(k, carry):
        pl.semaphore_signal(
            barrier, inc=1, device_id={"tile": lax.rem(me + k, tiles)}, device_id_type=pl.DeviceIdType.MESH
        )
        return carry

    lax.fori_loop(1, tiles, greet, 0)
    own_r = pltpu.make_async_copy(res, rn.at[:, pl.ds(MARGIN, planes)], loc_sem.at[0])
    own_c = pltpu.make_async_copy(coup, cn.at[pl.ds(MARGIN, planes)], loc_sem.at[1])
    own_r.start()
    own_c.start()

    @pl.when(me == 0)
    def _():
        rn[:, :MARGIN] = jnp.zeros_like(rn[:, :MARGIN])
        cn[:MARGIN] = jnp.zeros_like(cn[:MARGIN])
        hl[...] = jnp.zeros_like(hl)

    @pl.when(me == last)
    def _():
        rn[:, ext - MARGIN :] = jnp.zeros_like(rn[:, ext - MARGIN :])
        cn[ext - MARGIN :] = jnp.zeros_like(cn[ext - MARGIN :])
        ys[:, planes] = jnp.zeros_like(ys[:, planes])

    pl.semaphore_wait(barrier, tiles - 1)

    def remote(src, dst, send, recv, peer):
        return pltpu.make_async_remote_copy(
            src_ref=src, dst_ref=dst, send_sem=send, recv_sem=recv,
            device_id={"tile": peer}, device_id_type=pl.DeviceIdType.MESH,
        )

    left, right = lax.rem(me + tiles - 1, tiles), lax.rem(me + 1, tiles)
    tail, head = pl.ds(planes - MARGIN, MARGIN), pl.ds(0, MARGIN)
    low, high = pl.ds(0, MARGIN), pl.ds(ext - MARGIN, MARGIN)
    to_right = [
        remote(res.at[:, tail], rn.at[:, low], halo_send.at[0], halo_recv.at[0], right),
        remote(coup.at[tail], cn.at[low], halo_send.at[1], halo_recv.at[1], right),
    ]
    to_left = [
        remote(res.at[:, head], rn.at[:, high], halo_send.at[2], halo_recv.at[2], left),
        remote(coup.at[head], cn.at[high], halo_send.at[3], halo_recv.at[3], left),
    ]

    @pl.when(me < last)
    def _():
        for copy in to_right:
            copy.start()

    @pl.when(me > 0)
    def _():
        for copy in to_left:
            copy.start()

    xs[:, ext] = jnp.zeros_like(xs[:, ext])
    hs[:, 0] = jnp.zeros_like(hs[:, 0])

    def permuted(ref, *at):
        return jnp.concatenate([ref[(*at, pl.ds(v, 8, stride=groups), slice(None))] for v in range(groups)], axis=0)

    def put(ref, value, *at):
        for v in range(groups):
            ref[(*at, pl.ds(v, 8, stride=groups), slice(None))] = value[8 * v : 8 * v + 8]

    def prepare(p):
        c = permuted(cn, p)
        q = damping / (16.0 + c * c)
        a, b = 4.0 * q, c * q
        coef[0, p], coef[1, p], coef[2, p] = a, b, c
        for k in range(3):
            real, imag = permuted(rn, k, p), permuted(rn, k + 3, p)
            rhs[k, p], rhs[k + 3, p] = real, imag
            xs[k, p] = a * real + b * imag
            xs[k + 3, p] = a * imag - b * real

    own_r.wait()
    own_c.wait()
    for p in range(MARGIN, MARGIN + planes):
        prepare(p)

    cells = 6 * ny
    col = iota((8, cells), 1)
    row_in = lax.rem(col, ny)
    y_of = lax.rem(row_in, 8) * groups + row_in // 8
    chan = col // ny
    parity = lax.rem(y_of // 4, 2)
    keys = []
    for zb in range(zblocks):
        key = jnp.full((8, cells), -1, jnp.int32)
        for yb in range(ny // 8):
            b = yb * zblocks + zb
            value = jnp.where(earth[0, b] == 1, owners[0, b], -1)
            key = jnp.where(y_of // 8 == yb, value, key)
        keys.append(key)
    mine = chan == iota((8, cells), 0)
    sums = []
    for k in range(6):
        total = rhs[k, MARGIN]
        for p in range(MARGIN + 1, MARGIN + planes):
            total = total + rhs[k, p]
        sums.append(total)
    sums = jnp.concatenate(sums, axis=0)
    combos = [(par, zb) for par in range(2) for zb in range(zblocks)]

    def spread(par, zb, dims, weight):
        z, lane = iota((nz, 128), 0), iota((nz, 128), 1)
        if dims:
            z, lane = iota((128, nz), 1), iota((128, nz), 0)
        hit = (z // 64 == zb) & (lane == par * 16 + lax.rem(z, 64) // 4)
        return jnp.where(hit, weight, 0.0).astype(F32)

    def restrict(group, carry):
        for j, (par, zb) in enumerate(combos):
            for o in range(8):
                hit = mine & (parity == par) & (keys[zb] == group * 8 + o)
                w_ref[group, j * 64 + o * 8 : j * 64 + o * 8 + 8] = jnp.where(hit, 1.0, 0.0).astype(F32)
        partial = jnp.dot(w_ref[group], sums, precision=HIGH, preferred_element_type=F32)
        agg = jnp.zeros((64, 128), F32)
        for j, (par, zb) in enumerate(combos):
            agg = agg + jnp.dot(
                partial[j * 64 : j * 64 + 64], spread(par, zb, 0, 1.0 / 64.0), precision=HIGH, preferred_element_type=F32
            )
        for o in range(8):
            outbox[group * 8 + o] = agg[o * 8 : o * 8 + 8]
        return carry

    if tiles == 8:
        restrict(0, 0)
    else:
        lax.fori_loop(0, tiles // 8, restrict, 0)

    def send_sum(k, carry):
        peer = lax.rem(me + k, tiles)
        remote(outbox.at[peer], inbox.at[me], s1.at[k], r1.at[me], peer).start()
        return carry

    lax.fori_loop(1, tiles, send_sum, 0)
    inbox[me] = outbox[me]

    @pl.when(me > 0)
    def _():
        for copy in to_right:
            copy.wait_recv()

    for p in range(MARGIN):
        prepare(p)

    @pl.when(me < last)
    def _():
        for copy in to_left:
            copy.wait_recv()

    for p in range(ext - MARGIN, ext):
        prepare(p)

    def faces(src, p, f, ahead=True):
        ex, ey, ez = src[f, p], src[f + 1, p], src[f + 2, p]
        ney, nez = -ey, ez
        if ahead:
            ney, nez = src[f + 1, p + 1] - ey, ez - src[f + 2, p + 1]
        hx = (y_next(ez) - ez) - (z_next(ey) - ey)
        hy = (z_next(ex) - ex) + nez
        hz = ney - (y_next(ex) - ex)
        return hx, hy, hz

    def edge(src, p, f, k):
        if k == 0:
            hy, hz = src[f + 1, p + 1], src[f + 2, p + 1]
            return (hz - y_prev(hz)) - (hy - z_prev(hy))
        hx = src[f, p + 1]
        if k == 1:
            return (hx - z_prev(hx)) - (src[f + 2, p + 1] - src[f + 2, p])
        return (src[f + 1, p + 1] - src[f + 1, p]) - (hx - y_prev(hx))

    def all_faces(first, stop):
        for p in range(first, stop):
            for f in (0, 3):
                hs[f, p + 1], hs[f + 1, p + 1], hs[f + 2, p + 1] = faces(xs, p, f)

    count = sweeps[0]

    def update(p, active, store):
        c = coef[2, p]
        a, b = coef[0, p] * active, coef[1, p] * active
        for k in range(3):
            u, w = xs[k, p], xs[k + 3, p]
            real = rhs[k, p] - edge(hs, p, 0, k) + c * w
            imag = rhs[k + 3, p] - edge(hs, p, 3, k) - c * u
            store(k, p, u + (a * real + b * imag))
            store(k + 3, p, w + (a * imag - b * real))

    def keep(k, p, value):
        xs[k, p] = value

    def sweep(step, first, stop):
        active = jnp.where(step < count, 1.0, 0.0).astype(F32)
        all_faces(max(first - 1, 0), stop)
        for p in range(first, stop):
            update(p, active, keep)

    def full(step, carry):
        sweep(step, 0, ext)
        return carry

    cut = SWEEPS // 2
    lax.fori_loop(1, cut, full, 0)

    def wait_sum(k, carry):
        peer = lax.rem(me + k, tiles)
        done = remote(outbox.at[peer], inbox.at[peer], s1.at[k], r1.at[peer], peer)
        done.wait_send()
        done.wait_recv()
        return carry

    lax.fori_loop(1, tiles, wait_sum, 0)
    if tiles == 8:
        total = inbox[0]
        for t in range(1, tiles):
            total = total + inbox[t]
    else:
        total = lax.fori_loop(0, tiles, lambda t, acc: acc + inbox[t], jnp.zeros((8, 128), F32))
    width = inv.shape[0]
    fold = jnp.where(iota((128, width), 0) == lax.rem(iota((128, width), 1), 32), 1.0, 0.0).astype(F32)
    unfold = jnp.where(iota((width, 128), 1) == lax.rem(iota((width, 128), 0), 32), 1.0, 0.0).astype(F32)
    own_channel = iota((8, width), 0) == iota((8, width), 1) // 32
    flat = jnp.where(own_channel, jnp.dot(total, fold, precision=HIGH, preferred_element_type=F32), 0.0)
    flat = jnp.broadcast_to(jnp.sum(flat, axis=0, keepdims=True), (8, width))
    corr = lax.dot_general(flat, inv[...], (((1,), (1,)), ((), ())), precision=HIGH, preferred_element_type=F32)
    corr = jnp.where(own_channel, corr * scale[...], 0.0)
    csrc[...] = jnp.dot(corr, unfold, precision=HIGH, preferred_element_type=F32)

    def send_corr(k, carry):
        peer = lax.rem(me + k, tiles)
        remote(csrc, cbox.at[me], s2.at[k], r2.at[me], peer).start()
        return carry

    lax.fori_loop(1, tiles, send_corr, 0)
    cbox[me] = csrc[...]

    lax.fori_loop(cut, SWEEPS - 2, full, 0)
    sweep(SWEEPS - 2, MARGIN - 1, MARGIN + planes + 1)

    def wait_corr(k, carry):
        peer = lax.rem(me + k, tiles)
        done = remote(csrc, cbox.at[peer], s2.at[k], r2.at[peer], peer)
        done.wait_send()
        done.wait_recv()
        return carry

    lax.fori_loop(1, tiles, wait_corr, 0)
    fine[...] = jnp.zeros_like(fine)

    def prolong(group, carry):
        box = jnp.concatenate([cbox[group * 8 + o] for o in range(8)], axis=0)
        parts = [
            jnp.dot(box, spread(par, zb, 1, 1.0), precision=HIGH, preferred_element_type=F32) for par, zb in combos
        ]
        fine[...] += lax.dot_general(
            w_ref[group], jnp.concatenate(parts, axis=0), (((0,), (0,)), ((), ())),
            precision=HIGH, preferred_element_type=F32,
        )
        return carry

    if tiles == 8:
        prolong(0, 0)
    else:
        lax.fori_loop(0, tiles // 8, prolong, 0)

    active = jnp.where(SWEEPS - 1 < count, 1.0, 0.0).astype(F32)
    all_faces(MARGIN - 1, MARGIN + planes)

    def finish(k, p, value):
        value = value + fine[k * ny : k * ny + ny]
        ys[k, p - MARGIN] = value
        put(pn, value, k, p - MARGIN)

    update(MARGIN + planes - 1, active, finish)
    for i, f in enumerate((0, 3)):
        hx, hy, hz = faces(ys, planes - 1, f, ahead=False)
        gx[i], gs[2 * i], gs[2 * i + 1] = hx, hy, hz
    exit_right = [remote(gs, hl, fs.at[0], fr.at[0], right)]

    @pl.when(me < last)
    def _():
        for copy in exit_right:
            copy.start()

    update(MARGIN, active, finish)
    exit_left = [
        remote(ys.at[lo:hi, 0], ys.at[lo:hi, planes], fs.at[1 + i], fr.at[1 + i], left)
        for i, (lo, hi) in enumerate(SPLIT)
    ]

    @pl.when(me > 0)
    def _():
        for copy in exit_left:
            copy.start()

    for p in range(MARGIN + 1, MARGIN + planes - 1):
        update(p, active, finish)
    out_pre = pltpu.make_async_copy(pn, pre, out_sem.at[0])
    out_pre.start()
    for p in range(planes - 1):
        for f in (0, 3):
            hs[f, p + 1], hs[f + 1, p + 1], hs[f + 2, p + 1] = faces(ys, p, f)

    def image(p):
        c = coef[2, p + MARGIN]
        for k in range(3):
            put(qn, edge(hs, p, 0, k) - c * ys[k + 3, p], k, p)
            put(qn, edge(hs, p, 3, k) + c * ys[k, p], k + 3, p)

    for p in range(1, planes - 1):
        image(p)

    @pl.when(me > 0)
    def _():
        for copy in exit_right:
            copy.wait_recv()

    leading = jnp.where(me > 0, 1.0, 0.0).astype(F32)
    for i, f in enumerate((0, 3)):
        hs[f + 1, 0] = (hl[2 * i] - ys[f + 2, 0]) * leading
        hs[f + 2, 0] = (hl[2 * i + 1] + ys[f + 1, 0]) * leading
    image(0)

    @pl.when(me < last)
    def _():
        for copy in exit_left:
            copy.wait_recv()

    for i, f in enumerate((0, 3)):
        hs[f, planes] = gx[i]
        hs[f + 1, planes] = gs[2 * i] - ys[f + 2, planes]
        hs[f + 2, planes] = gs[2 * i + 1] + ys[f + 1, planes]
    image(planes - 1)
    out_img = pltpu.make_async_copy(qn, img, out_sem.at[1])
    out_img.start()

    @pl.when(me < last)
    def _():
        for copy in to_right + exit_right:
            copy.wait_send()

    @pl.when(me > 0)
    def _():
        for copy in to_left + exit_left:
            copy.wait_send()

    out_pre.wait()
    out_img.wait()


def shards(residual, coupling, owners, earth, sweep_counts, coarse_inverse, coarse_scale):
    tiles = lax.axis_size("tile")
    chans, planes, ny, nz = residual.shape
    ext = planes + 2 * MARGIN
    groups = -(-tiles // 8)
    wide = 2 * (nz // 64) * 64

    def field(*lead):
        return pltpu.VMEM((*lead, ny, nz), F32)

    vmem = pl.BlockSpec(memory_space=pltpu.VMEM)
    smem = pl.BlockSpec(memory_space=pltpu.SMEM)
    hbm = pl.BlockSpec(memory_space=pl.ANY)
    dma = pltpu.SemaphoreType.DMA
    shape = jax.ShapeDtypeStruct(residual.shape, F32)
    return pl.pallas_call(
        functools.partial(kernel, tiles),
        out_shape=(shape, shape),
        in_specs=[hbm, hbm, smem, smem, smem, vmem, vmem],
        out_specs=(hbm, hbm),
        scratch_shapes=[
            field(chans, ext),
            field(ext),
            field(chans, ext),
            field(3, ext),
            field(chans, ext + 1),
            field(chans, ext + 1),
            field(chans, planes + 1),
            field(4),
            field(2),
            field(4),
            pltpu.VMEM((chans * ny, nz), F32),
            field(chans, planes),
            field(chans, planes),
            pltpu.VMEM((groups, wide, chans * ny), F32),
            pltpu.VMEM((groups * 8, 8, 128), F32),
            pltpu.VMEM((groups * 8, 8, 128), F32),
            pltpu.VMEM((groups * 8, 8, 128), F32),
            pltpu.VMEM((8, 128), F32),
            dma((2,)), dma((4,)), dma((4,)),
            dma((tiles,)), dma((tiles,)), dma((tiles,)), dma((tiles,)),
            dma((3,)), dma((3,)), dma((2,)),
        ],
        compiler_params=pltpu.CompilerParams(
            collective_id=0, has_side_effects=True, vmem_limit_bytes=48 * 1024 * 1024
        ),
        name="schwarz",
    )(residual, coupling, owners, earth, sweep_counts, coarse_inverse, coarse_scale)


def solution(mesh):
    return jax.shard_map(
        shards,
        mesh=mesh,
        in_specs=(
            P("pair", "tile", None, None),
            P("tile", "pair", None),
            P("tile", None),
            P("tile", None),
            P("tile"),
            P("pair", None),
            P("tile", "pair"),
        ),
        out_specs=(P("pair", "tile", None, None), P("pair", "tile", None, None)),
        check_vma=False,
    )
```

```python
import functools

import jax
import jax.numpy as jnp
from jax import lax
from jax.experimental import pallas as pl
from jax.experimental.pallas import tpu as pltpu
from jax.sharding import PartitionSpec as P

MARGIN = 2
SWEEPS = 8
damping = 0.4
HIGH = lax.Precision.HIGHEST
F32 = jnp.float32
SPLIT = ((1, 3), (4, 6))


def iota(shape, dim):
    return lax.broadcasted_iota(jnp.int32, shape, dim)


def z_next(x):
    width = x.shape[1]
    return jnp.where(iota(x.shape, 1) < width - 1, pltpu.roll(x, width - 1, 1), 0.0)


def z_prev(x):
    return jnp.where(iota(x.shape, 1) > 0, pltpu.roll(x, 1, 1), 0.0)


def y_next(x):
    edge = x[:8]
    edge = jnp.where(iota(edge.shape, 0) < 7, pltpu.roll(edge, 7, 0), 0.0)
    return jnp.concatenate([x[8:], edge], axis=0)


def y_prev(x):
    rows = x.shape[0]
    edge = x[rows - 8 :]
    edge = jnp.where(iota(edge.shape, 0) > 0, pltpu.roll(edge, 1, 0), 0.0)
    return jnp.concatenate([edge, x[: rows - 8]], axis=0)


def kernel(
    tiles,
    res, coup, owners_in, earth_in, sweeps_in, inv_in, scale_in,
    pre, img,
    owners, earth, sweeps, inv, scale,
    rn, cn, rhs, coef, xs, hs, ys, gs, gx, hl, fine, w_ref, outbox, inbox, cbox, csrc,
    loc_sem, halo_send, halo_recv, s1, r1, s2, r2, fs, fr,
):
    me = lax.axis_index("tile")
    planes = res.shape[1]
    ny, nz = res.shape[2], res.shape[3]
    groups = ny // 8
    ext = planes + 2 * MARGIN
    zblocks = nz // 64
    last = tiles - 1

    barrier = pltpu.get_barrier_semaphore()

    def greet(k, carry):
        pl.semaphore_signal(
            barrier, inc=1, device_id={"tile": lax.rem(me + k, tiles)}, device_id_type=pl.DeviceIdType.MESH
        )
        return carry

    lax.fori_loop(1, tiles, greet, 0)
    own_r = pltpu.make_async_copy(res, rn.at[:, pl.ds(MARGIN, planes)], loc_sem.at[0])
    own_c = pltpu.make_async_copy(coup, cn.at[pl.ds(MARGIN, planes)], loc_sem.at[1])
    own_r.start()
    own_c.start()
    small = [
        pltpu.make_async_copy(src, dst, loc_sem.at[2 + i])
        for i, (src, dst) in enumerate(
            ((owners_in, owners), (earth_in, earth), (sweeps_in, sweeps), (inv_in, inv), (scale_in, scale))
        )
    ]
    for copy in small:
        copy.start()

    @pl.when(me == 0)
    def _():
        rn[:, :MARGIN] = jnp.zeros_like(rn[:, :MARGIN])
        cn[:MARGIN] = jnp.zeros_like(cn[:MARGIN])
        hl[...] = jnp.zeros_like(hl)

    @pl.when(me == last)
    def _():
        rn[:, ext - MARGIN :] = jnp.zeros_like(rn[:, ext - MARGIN :])
        cn[ext - MARGIN :] = jnp.zeros_like(cn[ext - MARGIN :])
        ys[:, planes] = jnp.zeros_like(ys[:, planes])

    pl.semaphore_wait(barrier, tiles - 1)

    def remote(src, dst, send, recv, peer):
        return pltpu.make_async_remote_copy(
            src_ref=src, dst_ref=dst, send_sem=send, recv_sem=recv,
            device_id={"tile": peer}, device_id_type=pl.DeviceIdType.MESH,
        )

    left, right = lax.rem(me + tiles - 1, tiles), lax.rem(me + 1, tiles)
    tail, head = pl.ds(planes - MARGIN, MARGIN), pl.ds(0, MARGIN)
    low, high = pl.ds(0, MARGIN), pl.ds(ext - MARGIN, MARGIN)
    to_right = [
        remote(res.at[:, tail], rn.at[:, low], halo_send.at[0], halo_recv.at[0], right),
        remote(coup.at[tail], cn.at[low], halo_send.at[1], halo_recv.at[1], right),
    ]
    to_left = [
        remote(res.at[:, head], rn.at[:, high], halo_send.at[2], halo_recv.at[2], left),
        remote(coup.at[head], cn.at[high], halo_send.at[3], halo_recv.at[3], left),
    ]

    @pl.when(me < last)
    def _():
        for copy in to_right:
            copy.start()

    @pl.when(me > 0)
    def _():
        for copy in to_left:
            copy.start()

    xs[:, ext] = jnp.zeros_like(xs[:, ext])
    hs[:, 0] = jnp.zeros_like(hs[:, 0])

    def permuted(ref, *at):
        return jnp.concatenate([ref[(*at, pl.ds(v, 8, stride=groups), slice(None))] for v in range(groups)], axis=0)

    def put(ref, value, *at):
        for v in range(groups):
            ref[(*at, pl.ds(v, 8, stride=groups), slice(None))] = value[8 * v : 8 * v + 8]

    def prepare(p):
        c = permuted(cn, p)
        q = damping / (16.0 + c * c)
        a, b = 4.0 * q, c * q
        coef[0, p], coef[1, p], coef[2, p] = a, b, c
        for k in range(3):
            real, imag = permuted(rn, k, p), permuted(rn, k + 3, p)
            rhs[k, p], rhs[k + 3, p] = real, imag
            xs[k, p] = a * real + b * imag
            xs[k + 3, p] = a * imag - b * real

    own_r.wait()
    own_c.wait()
    for p in range(MARGIN, MARGIN + planes):
        prepare(p)

    for copy in small:
        copy.wait()

    cells = 6 * ny
    col = iota((8, cells), 1)
    row_in = lax.rem(col, ny)
    y_of = lax.rem(row_in, 8) * groups + row_in // 8
    chan = col // ny
    parity = lax.rem(y_of // 4, 2)
    keys = []
    for zb in range(zblocks):
        key = jnp.full((8, cells), -1, jnp.int32)
        for yb in range(ny // 8):
            b = yb * zblocks + zb
            value = jnp.where(earth[0, b] == 1, owners[0, b], -1)
            key = jnp.where(y_of // 8 == yb, value, key)
        keys.append(key)
    mine = chan == iota((8, cells), 0)
    sums = []
    for k in range(6):
        total = rhs[k, MARGIN]
        for p in range(MARGIN + 1, MARGIN + planes):
            total = total + rhs[k, p]
        sums.append(total)
    sums = jnp.concatenate(sums, axis=0)
    combos = [(par, zb) for par in range(2) for zb in range(zblocks)]

    def spread(par, zb, dims, weight):
        z, lane = iota((nz, 128), 0), iota((nz, 128), 1)
        if dims:
            z, lane = iota((128, nz), 1), iota((128, nz), 0)
        hit = (z // 64 == zb) & (lane == par * 16 + lax.rem(z, 64) // 4)
        return jnp.where(hit, weight, 0.0).astype(F32)

    def restrict(group, carry):
        for j, (par, zb) in enumerate(combos):
            for o in range(8):
                hit = mine & (parity == par) & (keys[zb] == group * 8 + o)
                w_ref[group, j * 64 + o * 8 : j * 64 + o * 8 + 8] = jnp.where(hit, 1.0, 0.0).astype(F32)
        partial = jnp.dot(w_ref[group], sums, precision=HIGH, preferred_element_type=F32)
        agg = jnp.zeros((64, 128), F32)
        for j, (par, zb) in enumerate(combos):
            agg = agg + jnp.dot(
                partial[j * 64 : j * 64 + 64], spread(par, zb, 0, 1.0 / 64.0), precision=HIGH, preferred_element_type=F32
            )
        for o in range(8):
            outbox[group * 8 + o] = agg[o * 8 : o * 8 + 8]
        return carry

    if tiles == 8:
        restrict(0, 0)
    else:
        lax.fori_loop(0, tiles // 8, restrict, 0)

    def send_sum(k, carry):
        peer = lax.rem(me + k, tiles)
        remote(outbox.at[peer], inbox.at[me], s1.at[k], r1.at[me], peer).start()
        return carry

    lax.fori_loop(1, tiles, send_sum, 0)
    inbox[me] = outbox[me]

    @pl.when(me > 0)
    def _():
        for copy in to_right:
            copy.wait_recv()

    for p in range(MARGIN):
        prepare(p)

    @pl.when(me < last)
    def _():
        for copy in to_left:
            copy.wait_recv()

    for p in range(ext - MARGIN, ext):
        prepare(p)

    def faces(src, p, f, ahead=True):
        ex, ey, ez = src[f, p], src[f + 1, p], src[f + 2, p]
        ney, nez = -ey, ez
        if ahead:
            ney, nez = src[f + 1, p + 1] - ey, ez - src[f + 2, p + 1]
        hx = (y_next(ez) - ez) - (z_next(ey) - ey)
        hy = (z_next(ex) - ex) + nez
        hz = ney - (y_next(ex) - ex)
        return hx, hy, hz

    def edge(src, p, f, k):
        if k == 0:
            hy, hz = src[f + 1, p + 1], src[f + 2, p + 1]
            return (hz - y_prev(hz)) - (hy - z_prev(hy))
        hx = src[f, p + 1]
        if k == 1:
            return (hx - z_prev(hx)) - (src[f + 2, p + 1] - src[f + 2, p])
        return (src[f + 1, p + 1] - src[f + 1, p]) - (hx - y_prev(hx))

    def all_faces(first, stop):
        for p in range(first, stop):
            for f in (0, 3):
                hs[f, p + 1], hs[f + 1, p + 1], hs[f + 2, p + 1] = faces(xs, p, f)

    count = sweeps[0, 0]

    def update(p, active, store):
        c = coef[2, p]
        a, b = coef[0, p] * active, coef[1, p] * active
        for k in range(3):
            u, w = xs[k, p], xs[k + 3, p]
            real = rhs[k, p] - edge(hs, p, 0, k) + c * w
            imag = rhs[k + 3, p] - edge(hs, p, 3, k) - c * u
            store(k, p, u + (a * real + b * imag))
            store(k + 3, p, w + (a * imag - b * real))

    def keep(k, p, value):
        xs[k, p] = value

    def sweep(step, first, stop):
        active = jnp.where(step < count, 1.0, 0.0).astype(F32)
        all_faces(max(first - 1, 0), stop)
        for p in range(first, stop):
            update(p, active, keep)

    def full(step, carry):
        sweep(step, 0, ext)
        return carry

    cut = SWEEPS // 2
    lax.fori_loop(1, cut, full, 0)

    def wait_sum(k, carry):
        peer = lax.rem(me + k, tiles)
        done = remote(outbox.at[peer], inbox.at[peer], s1.at[k], r1.at[peer], peer)
        done.wait_send()
        done.wait_recv()
        return carry

    lax.fori_loop(1, tiles, wait_sum, 0)
    if tiles == 8:
        total = inbox[0]
        for t in range(1, tiles):
            total = total + inbox[t]
    else:
        total = lax.fori_loop(0, tiles, lambda t, acc: acc + inbox[t], jnp.zeros((8, 128), F32))
    width = inv.shape[0]
    fold = jnp.where(iota((128, width), 0) == lax.rem(iota((128, width), 1), 32), 1.0, 0.0).astype(F32)
    unfold = jnp.where(iota((width, 128), 1) == lax.rem(iota((width, 128), 0), 32), 1.0, 0.0).astype(F32)
    own_channel = iota((8, width), 0) == iota((8, width), 1) // 32
    flat = jnp.where(own_channel, jnp.dot(total, fold, precision=HIGH, preferred_element_type=F32), 0.0)
    flat = jnp.broadcast_to(jnp.sum(flat, axis=0, keepdims=True), (8, width))
    corr = lax.dot_general(flat, inv[...], (((1,), (1,)), ((), ())), precision=HIGH, preferred_element_type=F32)
    corr = jnp.where(own_channel, corr * scale[...], 0.0)
    csrc[...] = jnp.dot(corr, unfold, precision=HIGH, preferred_element_type=F32)

    def send_corr(k, carry):
        peer = lax.rem(me + k, tiles)
        remote(csrc, cbox.at[me], s2.at[k], r2.at[me], peer).start()
        return carry

    lax.fori_loop(1, tiles, send_corr, 0)
    cbox[me] = csrc[...]

    lax.fori_loop(cut, SWEEPS - 2, full, 0)
    sweep(SWEEPS - 2, MARGIN - 1, MARGIN + planes + 1)

    def wait_corr(k, carry):
        peer = lax.rem(me + k, tiles)
        done = remote(csrc, cbox.at[peer], s2.at[k], r2.at[peer], peer)
        done.wait_send()
        done.wait_recv()
        return carry

    lax.fori_loop(1, tiles, wait_corr, 0)
    fine[...] = jnp.zeros_like(fine)

    def prolong(group, carry):
        box = jnp.concatenate([cbox[group * 8 + o] for o in range(8)], axis=0)
        parts = [
            jnp.dot(box, spread(par, zb, 1, 1.0), precision=HIGH, preferred_element_type=F32) for par, zb in combos
        ]
        fine[...] += lax.dot_general(
            w_ref[group], jnp.concatenate(parts, axis=0), (((0,), (0,)), ((), ())),
            precision=HIGH, preferred_element_type=F32,
        )
        return carry

    if tiles == 8:
        prolong(0, 0)
    else:
        lax.fori_loop(0, tiles // 8, prolong, 0)

    active = jnp.where(SWEEPS - 1 < count, 1.0, 0.0).astype(F32)
    all_faces(MARGIN - 1, MARGIN + planes)

    def finish(k, p, value):
        value = value + fine[k * ny : k * ny + ny]
        ys[k, p - MARGIN] = value
        put(pre, value, k, p - MARGIN)

    update(MARGIN + planes - 1, active, finish)
    for i, f in enumerate((0, 3)):
        hx, hy, hz = faces(ys, planes - 1, f, ahead=False)
        gx[i], gs[2 * i], gs[2 * i + 1] = hx, hy, hz
    exit_right = [remote(gs, hl, fs.at[0], fr.at[0], right)]

    @pl.when(me < last)
    def _():
        for copy in exit_right:
            copy.start()

    update(MARGIN, active, finish)
    exit_left = [
        remote(ys.at[lo:hi, 0], ys.at[lo:hi, planes], fs.at[1 + i], fr.at[1 + i], left)
        for i, (lo, hi) in enumerate(SPLIT)
    ]

    @pl.when(me > 0)
    def _():
        for copy in exit_left:
            copy.start()

    for p in range(MARGIN + 1, MARGIN + planes - 1):
        update(p, active, finish)
    for p in range(planes - 1):
        for f in (0, 3):
            hs[f, p + 1], hs[f + 1, p + 1], hs[f + 2, p + 1] = faces(ys, p, f)

    def image(p):
        c = coef[2, p + MARGIN]
        for k in range(3):
            put(img, edge(hs, p, 0, k) - c * ys[k + 3, p], k, p)
            put(img, edge(hs, p, 3, k) + c * ys[k, p], k + 3, p)

    for p in range(1, planes - 1):
        image(p)

    @pl.when(me > 0)
    def _():
        for copy in exit_right:
            copy.wait_recv()

    leading = jnp.where(me > 0, 1.0, 0.0).astype(F32)
    for i, f in enumerate((0, 3)):
        hs[f + 1, 0] = (hl[2 * i] - ys[f + 2, 0]) * leading
        hs[f + 2, 0] = (hl[2 * i + 1] + ys[f + 1, 0]) * leading
    image(0)

    @pl.when(me < last)
    def _():
        for copy in exit_left:
            copy.wait_recv()

    for i, f in enumerate((0, 3)):
        hs[f, planes] = gx[i]
        hs[f + 1, planes] = gs[2 * i] - ys[f + 2, planes]
        hs[f + 2, planes] = gs[2 * i + 1] + ys[f + 1, planes]
    image(planes - 1)

    @pl.when(me < last)
    def _():
        for copy in to_right + exit_right:
            copy.wait_send()

    @pl.when(me > 0)
    def _():
        for copy in to_left + exit_left:
            copy.wait_send()


def store(pre, img, pre_out, img_out, sem):
    copies = [pltpu.make_async_copy(pre, pre_out, sem.at[0]), pltpu.make_async_copy(img, img_out, sem.at[1])]
    for copy in copies:
        copy.start()
    for copy in copies:
        copy.wait()


def shards(residual, coupling, owners, earth, sweep_counts, coarse_inverse, coarse_scale):
    tiles = lax.axis_size("tile")
    chans, planes, ny, nz = residual.shape
    ext = planes + 2 * MARGIN
    groups = -(-tiles // 8)
    wide = 2 * (nz // 64) * 64

    def field(*lead):
        return pltpu.VMEM((*lead, ny, nz), F32)

    hbm = pl.BlockSpec(memory_space=pltpu.HBM)
    vmem = pl.BlockSpec(memory_space=pltpu.VMEM)
    dma = pltpu.SemaphoreType.DMA
    grant = 67043328 - 2 * residual.size * 4 - 64 * 1024
    sweep_counts = sweep_counts.reshape(1, 1)
    staged = pltpu.VMEM(residual.shape, F32)
    shape = jax.ShapeDtypeStruct(residual.shape, F32)
    outs = pl.pallas_call(
        functools.partial(kernel, tiles),
        out_shape=(staged, staged),
        in_specs=[hbm] * 7,
        out_specs=(vmem, vmem),
        scratch_shapes=[
            pltpu.SMEM(owners.shape, jnp.int32),
            pltpu.SMEM(earth.shape, jnp.int32),
            pltpu.SMEM(sweep_counts.shape, jnp.int32),
            pltpu.VMEM(coarse_inverse.shape, F32),
            pltpu.VMEM(coarse_scale.shape, F32),
            field(chans, ext),
            field(ext),
            field(chans, ext),
            field(3, ext),
            field(chans, ext + 1),
            field(chans, ext + 1),
            field(chans, planes + 1),
            field(4),
            field(2),
            field(4),
            pltpu.VMEM((chans * ny, nz), F32),
            pltpu.VMEM((groups, wide, chans * ny), F32),
            pltpu.VMEM((groups * 8, 8, 128), F32),
            pltpu.VMEM((groups * 8, 8, 128), F32),
            pltpu.VMEM((groups * 8, 8, 128), F32),
            pltpu.VMEM((8, 128), F32),
            dma((7,)), dma((4,)), dma((4,)),
            dma((tiles,)), dma((tiles,)), dma((tiles,)), dma((tiles,)),
            dma((3,)), dma((3,)),
        ],
        compiler_params=pltpu.CompilerParams(
            collective_id=0, has_side_effects=True, vmem_limit_bytes=grant
        ),
        name="schwarz",
    )(residual, coupling, owners, earth, sweep_counts, coarse_inverse, coarse_scale)
    return pl.pallas_call(
        store,
        out_shape=(shape, shape),
        in_specs=[vmem, vmem],
        out_specs=(hbm, hbm),
        scratch_shapes=[dma((2,))],
        compiler_params=pltpu.CompilerParams(vmem_limit_bytes=1024 * 1024),
        name="store",
    )(*outs)


def solution(mesh):
    return jax.shard_map(
        shards,
        mesh=mesh,
        in_specs=(
            P("pair", "tile", None, None),
            P("tile", "pair", None),
            P("tile", None),
            P("tile", None),
            P("tile"),
            P("pair", None),
            P("tile", "pair"),
        ),
        out_specs=(P("pair", "tile", None, None), P("pair", "tile", None, None)),
        check_vma=False,
    )
```

```python
import functools

import jax
import jax.numpy as jnp
from jax import lax
from jax.experimental import pallas as pl
from jax.experimental.pallas import tpu as pltpu
from jax.sharding import PartitionSpec as P

MARGIN = 2
SWEEPS = 8
damping = 0.4
HIGH = lax.Precision.HIGHEST
F32 = jnp.float32
SPLIT = ((1, 3), (4, 6))


def iota(shape, dim):
    return lax.broadcasted_iota(jnp.int32, shape, dim)


def z_next(x):
    width = x.shape[1]
    return jnp.where(iota(x.shape, 1) < width - 1, pltpu.roll(x, width - 1, 1), 0.0)


def z_prev(x):
    return jnp.where(iota(x.shape, 1) > 0, pltpu.roll(x, 1, 1), 0.0)


def y_next(x):
    edge = x[:8]
    edge = jnp.where(iota(edge.shape, 0) < 7, pltpu.roll(edge, 7, 0), 0.0)
    return jnp.concatenate([x[8:], edge], axis=0)


def y_prev(x):
    rows = x.shape[0]
    edge = x[rows - 8 :]
    edge = jnp.where(iota(edge.shape, 0) > 0, pltpu.roll(edge, 1, 0), 0.0)
    return jnp.concatenate([edge, x[: rows - 8]], axis=0)


def kernel(
    tiles,
    res, coup, owners_in, earth_in, sweeps_in, inv_in, scale_in,
    pre, img,
    owners, earth, sweeps, inv, scale,
    rn, cn, rhs, coef, xs, hs, ys, gs, gx, hl, fine, w_ref, outbox, inbox, cbox, csrc, sbox,
    loc_sem, halo_send, halo_recv, s1, r1, s2, r2, fs, fr,
):
    me = lax.axis_index("tile")
    planes = res.shape[1]
    ny, nz = res.shape[2], res.shape[3]
    groups = ny // 8
    ext = planes + 2 * MARGIN
    zblocks = nz // 64
    last = tiles - 1
    one_phase = tiles == 8

    barrier = pltpu.get_barrier_semaphore()

    def greet(k, carry):
        pl.semaphore_signal(
            barrier, inc=1, device_id={"tile": lax.rem(me + k, tiles)}, device_id_type=pl.DeviceIdType.MESH
        )
        return carry

    lax.fori_loop(1, tiles, greet, 0)
    own_r = pltpu.make_async_copy(res, rn.at[:, pl.ds(MARGIN, planes)], loc_sem.at[0])
    own_c = pltpu.make_async_copy(coup, cn.at[pl.ds(MARGIN, planes)], loc_sem.at[1])
    own_r.start()
    own_c.start()
    small = [
        pltpu.make_async_copy(src, dst, loc_sem.at[2 + i])
        for i, (src, dst) in enumerate(
            ((owners_in, owners), (earth_in, earth), (sweeps_in, sweeps), (inv_in, inv), (scale_in, scale))
        )
    ]
    for copy in small:
        copy.start()

    @pl.when(me == 0)
    def _():
        rn[:, :MARGIN] = jnp.zeros_like(rn[:, :MARGIN])
        cn[:MARGIN] = jnp.zeros_like(cn[:MARGIN])
        hl[...] = jnp.zeros_like(hl)

    @pl.when(me == last)
    def _():
        rn[:, ext - MARGIN :] = jnp.zeros_like(rn[:, ext - MARGIN :])
        cn[ext - MARGIN :] = jnp.zeros_like(cn[ext - MARGIN :])
        ys[:, planes] = jnp.zeros_like(ys[:, planes])

    def remote(src, dst, send, recv, peer):
        return pltpu.make_async_remote_copy(
            src_ref=src, dst_ref=dst, send_sem=send, recv_sem=recv,
            device_id={"tile": peer}, device_id_type=pl.DeviceIdType.MESH,
        )

    left, right = lax.rem(me + tiles - 1, tiles), lax.rem(me + 1, tiles)
    near_right, far_right, near_left, far_left = [], [], [], []
    for d in range(MARGIN):
        there, mirror = MARGIN - 1 - d, ext - MARGIN + d
        for copies, peer, here, lands in (
            (near_right if d == 0 else far_right, right, planes - 1 - d, there),
            (near_left if d == 0 else far_left, left, d, mirror),
        ):
            slot = 4 * d + (0 if peer is right else 2)
            copies.append(
                remote(res.at[:, here], rn.at[:, lands], halo_send.at[slot], halo_recv.at[slot], peer)
            )
            copies.append(
                remote(coup.at[here], cn.at[lands], halo_send.at[slot + 1], halo_recv.at[slot + 1], peer)
            )
    to_right, to_left = near_right + far_right, near_left + far_left

    def start(rightward, leftward):
        @pl.when(me < last)
        def _():
            for copy in rightward:
                copy.start()

        @pl.when(me > 0)
        def _():
            for copy in leftward:
                copy.start()

    xs[:, ext] = jnp.zeros_like(xs[:, ext])
    hs[:, 0] = jnp.zeros_like(hs[:, 0])

    def permuted(ref, *at):
        return jnp.concatenate([ref[(*at, pl.ds(v, 8, stride=groups), slice(None))] for v in range(groups)], axis=0)

    def put(ref, value, *at):
        for v in range(groups):
            ref[(*at, pl.ds(v, 8, stride=groups), slice(None))] = value[8 * v : 8 * v + 8]

    def prepare(p):
        c = permuted(cn, p)
        q = damping / (16.0 + c * c)
        a, b = 4.0 * q, c * q
        coef[0, p], coef[1, p], coef[2, p] = a, b, c
        for k in range(3):
            real, imag = permuted(rn, k, p), permuted(rn, k + 3, p)
            rhs[k, p], rhs[k + 3, p] = real, imag
            xs[k, p] = a * real + b * imag
            xs[k + 3, p] = a * imag - b * real

    for copy in small:
        copy.wait()

    cells = 6 * ny
    col = iota((8, cells), 1)
    row_in = lax.rem(col, ny)
    y_of = lax.rem(row_in, 8) * groups + row_in // 8
    chan = col // ny
    parity = lax.rem(y_of // 4, 2)
    keys = []
    for zb in range(zblocks):
        key = jnp.full((8, cells), -1, jnp.int32)
        for yb in range(ny // 8):
            b = yb * zblocks + zb
            value = jnp.where(earth[0, b] == 1, owners[0, b], -1)
            key = jnp.where(y_of // 8 == yb, value, key)
        keys.append(key)
    mine = chan == iota((8, cells), 0)
    combos = [(par, zb) for par in range(2) for zb in range(zblocks)]

    def spread(par, zb, flip, weight, lanes):
        z, lane = iota((nz, lanes), 0), iota((nz, lanes), 1)
        if flip:
            z, lane = iota((lanes, nz), 1), iota((lanes, nz), 0)
        lane = lax.rem(lane, 32) if one_phase else lane
        hit = (z // 64 == zb) & (lane == par * 16 + lax.rem(z, 64) // 4)
        return jnp.where(hit, weight, 0.0).astype(F32)

    def mark(group, carry):
        for j, (par, zb) in enumerate(combos):
            for o in range(8):
                hit = mine & (parity == par) & (keys[zb] == group * 8 + o)
                w_ref[group, j * 64 + o * 8 : j * 64 + o * 8 + 8] = jnp.where(hit, 1.0, 0.0).astype(F32)
        return carry

    if one_phase:
        mark(0, 0)
    else:
        lax.fori_loop(0, tiles // 8, mark, 0)
    own_r.wait()
    own_c.wait()
    pl.semaphore_wait(barrier, tiles - 1)
    start(near_right, near_left)

    sums = []
    for k in range(6):
        total = permuted(rn, k, MARGIN)
        for p in range(MARGIN + 1, MARGIN + planes):
            total = total + permuted(rn, k, p)
        sums.append(total)
    sums = jnp.concatenate(sums, axis=0)
    wide = inbox.shape[2]

    def dot(x, y):
        return jnp.dot(x, y, precision=HIGH, preferred_element_type=F32)

    def restrict(group, carry):
        partial = dot(w_ref[group], sums)
        agg = jnp.zeros((64, wide), F32)
        for j, (par, zb) in enumerate(combos):
            agg = agg + dot(partial[j * 64 : j * 64 + 64], spread(par, zb, False, 1.0 / 64.0, wide))
        if one_phase:
            outbox[0] = dot(gather_rows, jnp.where(own_slot, agg, 0.0))
        else:
            for o in range(8):
                outbox[group * 8 + o] = agg[o * 8 : o * 8 + 8]
        return carry

    own_slot = lax.rem(iota((64, wide), 0), 8) == iota((64, wide), 1) // 32
    gather_rows = jnp.where(iota((8, 64), 0) == iota((8, 64), 1) // 8, 1.0, 0.0).astype(F32)
    if one_phase:
        restrict(0, 0)
    else:
        lax.fori_loop(0, tiles // 8, restrict, 0)

    def sum_copy(k, source):
        peer = lax.rem(me + k, tiles)
        slot = peer if source else me
        box = outbox.at[0] if one_phase else outbox.at[peer]
        return remote(box, inbox.at[slot], s1.at[k], r1.at[slot], peer)

    def scale_copy(k, source):
        peer = lax.rem(me + k, tiles)
        slot = peer if source else me
        return remote(scale_in, sbox.at[slot], s2.at[k], r2.at[slot], peer)

    def send_sum(k, carry):
        sum_copy(k, False).start()
        if one_phase:
            scale_copy(k, False).start()
        return carry

    lax.fori_loop(1, tiles, send_sum, 0)
    start(far_right, far_left)
    if one_phase:
        inbox[me] = outbox[0]
        sbox[me] = scale[...]
    else:
        inbox[me] = outbox[me]

    for p in range(MARGIN, MARGIN + planes):
        prepare(p)

    def wait_sum(k, carry):
        copies = [sum_copy(k, True)] + ([scale_copy(k, True)] if one_phase else [])
        for done in copies:
            done.wait_send()
            done.wait_recv()
        return carry

    def prolong(group, carry):
        if one_phase:
            total = inbox[0]
            for t in range(1, tiles):
                total = total + inbox[t]
            width = inv.shape[0]
            corr = lax.dot_general(
                total[:, :width], inv[...], (((1,), (1,)), ((), ())), precision=HIGH, preferred_element_type=F32
            )
            corr = corr * jnp.concatenate([sbox[t] for t in range(tiles)], axis=0)
            rows, lanes = iota((64, width), 0), iota((64, width), 1)
            copy_rows = jnp.where(iota((64, 8), 0) // 8 == iota((64, 8), 1), 1.0, 0.0).astype(F32)
            box = jnp.where(lax.rem(rows, 8) == lanes // 32, dot(copy_rows, corr), 0.0)
        else:
            width = 128
            box = jnp.concatenate([cbox[group * 8 + o] for o in range(8)], axis=0)
        parts = [dot(box, spread(par, zb, True, 1.0, width)) for par, zb in combos]
        value = lax.dot_general(
            w_ref[group], jnp.concatenate(parts, axis=0), (((0,), (0,)), ((), ())),
            precision=HIGH, preferred_element_type=F32,
        )
        fine[...] = value if one_phase else fine[...] + value
        return carry

    if one_phase:
        lax.fori_loop(1, tiles, wait_sum, 0)
        prolong(0, 0)

    @pl.when(me > 0)
    def _():
        for copy in to_right:
            copy.wait_recv()

    for p in range(MARGIN):
        prepare(p)

    @pl.when(me < last)
    def _():
        for copy in to_left:
            copy.wait_recv()

    for p in range(ext - MARGIN, ext):
        prepare(p)

    def faces(src, p, f, ahead=True):
        ex, ey, ez = src[f, p], src[f + 1, p], src[f + 2, p]
        ney, nez = -ey, ez
        if ahead:
            ney, nez = src[f + 1, p + 1] - ey, ez - src[f + 2, p + 1]
        hx = (y_next(ez) - ez) - (z_next(ey) - ey)
        hy = (z_next(ex) - ex) + nez
        hz = ney - (y_next(ex) - ex)
        return hx, hy, hz

    def edge(src, p, f, k):
        if k == 0:
            hy, hz = src[f + 1, p + 1], src[f + 2, p + 1]
            return (hz - y_prev(hz)) - (hy - z_prev(hy))
        hx = src[f, p + 1]
        if k == 1:
            return (hx - z_prev(hx)) - (src[f + 2, p + 1] - src[f + 2, p])
        return (src[f + 1, p + 1] - src[f + 1, p]) - (hx - y_prev(hx))

    def all_faces(first, stop):
        for p in range(first, stop):
            for f in (0, 3):
                hs[f, p + 1], hs[f + 1, p + 1], hs[f + 2, p + 1] = faces(xs, p, f)

    count = sweeps[0, 0]

    def update(p, active, store):
        c = coef[2, p]
        a, b = coef[0, p] * active, coef[1, p] * active
        for k in range(3):
            u, w = xs[k, p], xs[k + 3, p]
            real = rhs[k, p] - edge(hs, p, 0, k) + c * w
            imag = rhs[k + 3, p] - edge(hs, p, 3, k) - c * u
            store(k, p, u + (a * real + b * imag))
            store(k + 3, p, w + (a * imag - b * real))

    def keep(k, p, value):
        xs[k, p] = value

    def sweep(step, first, stop):
        active = jnp.where(step < count, 1.0, 0.0).astype(F32)
        all_faces(max(first - 1, 0), stop)
        for p in range(first, stop):
            update(p, active, keep)

    def full(step, carry):
        sweep(step, 0, ext)
        return carry

    cut = SWEEPS // 2
    lax.fori_loop(1, cut, full, 0)
    if not one_phase:
        lax.fori_loop(1, tiles, wait_sum, 0)
        total = lax.fori_loop(0, tiles, lambda t, acc: acc + inbox[t], jnp.zeros((8, 128), F32))
        width = inv.shape[0]
        fold = jnp.where(iota((128, width), 0) == lax.rem(iota((128, width), 1), 32), 1.0, 0.0).astype(F32)
        unfold = jnp.where(iota((width, 128), 1) == lax.rem(iota((width, 128), 0), 32), 1.0, 0.0).astype(F32)
        own_channel = iota((8, width), 0) == iota((8, width), 1) // 32
        flat = jnp.where(own_channel, jnp.dot(total, fold, precision=HIGH, preferred_element_type=F32), 0.0)
        flat = jnp.broadcast_to(jnp.sum(flat, axis=0, keepdims=True), (8, width))
        corr = lax.dot_general(flat, inv[...], (((1,), (1,)), ((), ())), precision=HIGH, preferred_element_type=F32)
        corr = jnp.where(own_channel, corr * scale[...], 0.0)
        csrc[...] = jnp.dot(corr, unfold, precision=HIGH, preferred_element_type=F32)

        def send_corr(k, carry):
            peer = lax.rem(me + k, tiles)
            remote(csrc, cbox.at[me], s2.at[k], r2.at[me], peer).start()
            return carry

        lax.fori_loop(1, tiles, send_corr, 0)
        cbox[me] = csrc[...]

    lax.fori_loop(cut, SWEEPS - 2, full, 0)
    sweep(SWEEPS - 2, MARGIN - 1, MARGIN + planes + 1)

    if not one_phase:

        def wait_corr(k, carry):
            peer = lax.rem(me + k, tiles)
            done = remote(csrc, cbox.at[peer], s2.at[k], r2.at[peer], peer)
            done.wait_send()
            done.wait_recv()
            return carry

        lax.fori_loop(1, tiles, wait_corr, 0)
        fine[...] = jnp.zeros_like(fine)

        lax.fori_loop(0, tiles // 8, prolong, 0)

    active = jnp.where(SWEEPS - 1 < count, 1.0, 0.0).astype(F32)
    all_faces(MARGIN + planes - 2, MARGIN + planes)

    def finish(k, p, value):
        value = value + fine[k * ny : k * ny + ny]
        ys[k, p - MARGIN] = value
        put(pre, value, k, p - MARGIN)

    update(MARGIN + planes - 1, active, finish)
    for i, f in enumerate((0, 3)):
        hx, hy, hz = faces(ys, planes - 1, f, ahead=False)
        gx[i], gs[2 * i], gs[2 * i + 1] = hx, hy, hz
    exit_right = [remote(gs, hl, fs.at[0], fr.at[0], right)]

    @pl.when(me < last)
    def _():
        for copy in exit_right:
            copy.start()

    all_faces(MARGIN - 1, MARGIN + planes - 2)
    update(MARGIN, active, finish)
    exit_left = [
        remote(ys.at[lo:hi, 0], ys.at[lo:hi, planes], fs.at[1 + i], fr.at[1 + i], left)
        for i, (lo, hi) in enumerate(SPLIT)
    ]

    @pl.when(me > 0)
    def _():
        for copy in exit_left:
            copy.start()

    for p in range(MARGIN + 1, MARGIN + planes - 1):
        update(p, active, finish)
    for p in range(planes - 1):
        for f in (0, 3):
            hs[f, p + 1], hs[f + 1, p + 1], hs[f + 2, p + 1] = faces(ys, p, f)

    def image(p):
        c = coef[2, p + MARGIN]
        for k in range(3):
            put(img, edge(hs, p, 0, k) - c * ys[k + 3, p], k, p)
            put(img, edge(hs, p, 3, k) + c * ys[k, p], k + 3, p)

    for p in range(1, planes - 1):
        image(p)

    @pl.when(me > 0)
    def _():
        for copy in exit_right:
            copy.wait_recv()

    leading = jnp.where(me > 0, 1.0, 0.0).astype(F32)
    for i, f in enumerate((0, 3)):
        hs[f + 1, 0] = (hl[2 * i] - ys[f + 2, 0]) * leading
        hs[f + 2, 0] = (hl[2 * i + 1] + ys[f + 1, 0]) * leading
    image(0)

    @pl.when(me < last)
    def _():
        for copy in exit_left:
            copy.wait_recv()

    for i, f in enumerate((0, 3)):
        hs[f, planes] = gx[i]
        hs[f + 1, planes] = gs[2 * i] - ys[f + 2, planes]
        hs[f + 2, planes] = gs[2 * i + 1] + ys[f + 1, planes]
    image(planes - 1)

    @pl.when(me < last)
    def _():
        for copy in to_right + exit_right:
            copy.wait_send()

    @pl.when(me > 0)
    def _():
        for copy in to_left + exit_left:
            copy.wait_send()


def store(pre, img, pre_out, img_out, sem):
    copies = [pltpu.make_async_copy(pre, pre_out, sem.at[0]), pltpu.make_async_copy(img, img_out, sem.at[1])]
    for copy in copies:
        copy.start()
    for copy in copies:
        copy.wait()


def shards(residual, coupling, owners, earth, sweep_counts, coarse_inverse, coarse_scale):
    tiles = lax.axis_size("tile")
    chans, planes, ny, nz = residual.shape
    ext = planes + 2 * MARGIN
    groups = -(-tiles // 8)
    wide = 2 * (nz // 64) * 64

    def field(*lead):
        return pltpu.VMEM((*lead, ny, nz), F32)

    hbm = pl.BlockSpec(memory_space=pltpu.HBM)
    vmem = pl.BlockSpec(memory_space=pltpu.VMEM)
    dma = pltpu.SemaphoreType.DMA
    grant = 67043328 - 2 * residual.size * 4 - 64 * 1024
    sweep_counts = sweep_counts.reshape(1, 1)
    staged = pltpu.VMEM(residual.shape, F32)
    shape = jax.ShapeDtypeStruct(residual.shape, F32)
    outs = pl.pallas_call(
        functools.partial(kernel, tiles),
        out_shape=(staged, staged),
        in_specs=[hbm] * 7,
        out_specs=(vmem, vmem),
        scratch_shapes=[
            pltpu.SMEM(owners.shape, jnp.int32),
            pltpu.SMEM(earth.shape, jnp.int32),
            pltpu.SMEM(sweep_counts.shape, jnp.int32),
            pltpu.VMEM(coarse_inverse.shape, F32),
            pltpu.VMEM(coarse_scale.shape, F32),
            field(chans, ext),
            field(ext),
            field(chans, ext),
            field(3, ext),
            field(chans, ext + 1),
            field(chans, ext + 1),
            field(chans, planes + 1),
            field(4),
            field(2),
            field(4),
            pltpu.VMEM((chans * ny, nz), F32),
            pltpu.VMEM((groups, wide, chans * ny), F32),
            pltpu.VMEM((groups * 8, 8, 256 if tiles == 8 else 128), F32),
            pltpu.VMEM((groups * 8, 8, 256 if tiles == 8 else 128), F32),
            pltpu.VMEM((groups * 8, 8, 128), F32),
            pltpu.VMEM((8, 128), F32),
            pltpu.VMEM((tiles, *coarse_scale.shape), F32),
            dma((7,)), dma((8,)), dma((8,)),
            dma((tiles,)), dma((tiles,)), dma((tiles,)), dma((tiles,)),
            dma((3,)), dma((3,)),
        ],
        compiler_params=pltpu.CompilerParams(
            collective_id=0, has_side_effects=True, vmem_limit_bytes=grant
        ),
        name="schwarz",
    )(residual, coupling, owners, earth, sweep_counts, coarse_inverse, coarse_scale)
    return pl.pallas_call(
        store,
        out_shape=(shape, shape),
        in_specs=[vmem, vmem],
        out_specs=(hbm, hbm),
        scratch_shapes=[dma((2,))],
        compiler_params=pltpu.CompilerParams(vmem_limit_bytes=1024 * 1024),
        name="store",
    )(*outs)


def solution(mesh):
    return jax.shard_map(
        shards,
        mesh=mesh,
        in_specs=(
            P("pair", "tile", None, None),
            P("tile", "pair", None),
            P("tile", None),
            P("tile", None),
            P("tile"),
            P("pair", None),
            P("tile", "pair"),
        ),
        out_specs=(P("pair", "tile", None, None), P("pair", "tile", None, None)),
        check_vma=False,
    )
```

```python
import functools

import jax
import jax.numpy as jnp
from jax import lax
from jax.experimental import pallas as pl
from jax.experimental.pallas import tpu as pltpu
from jax.sharding import PartitionSpec as P

MARGIN = 2
SWEEPS = 8
damping = 0.4
HIGH = lax.Precision.HIGHEST
F32 = jnp.float32
SPLIT = ((1, 3), (4, 6))


def iota(shape, dim):
    return lax.broadcasted_iota(jnp.int32, shape, dim)


def z_next(x):
    width = x.shape[1]
    return jnp.where(iota(x.shape, 1) < width - 1, pltpu.roll(x, width - 1, 1), 0.0)


def z_prev(x):
    return jnp.where(iota(x.shape, 1) > 0, pltpu.roll(x, 1, 1), 0.0)


def y_next(x):
    rows = x.shape[0]
    return jnp.where(iota(x.shape, 0) < rows - 1, pltpu.roll(x, rows - 1, 0), 0.0)


def y_prev(x):
    return jnp.where(iota(x.shape, 0) > 0, pltpu.roll(x, 1, 0), 0.0)


def kernel(
    tiles,
    res, coup, owners_in, earth_in, sweeps_in, inv_in, scale_in,
    pre, img,
    owners, earth, sweeps, inv, scale,
    rn, cn, coef, xs, hs, ys, gs, gx, hl, fine, w_ref, outbox, inbox, cbox, csrc, sbox,
    loc_sem, halo_send, halo_recv, s1, r1, s2, r2, fs, fr,
):
    me = lax.axis_index("tile")
    planes = res.shape[1]
    ny, nz = res.shape[2], res.shape[3]
    ext = planes + 2 * MARGIN
    zblocks = nz // 64
    last = tiles - 1
    one_phase = tiles == 8

    barrier = pltpu.get_barrier_semaphore()

    def greet(k, carry):
        pl.semaphore_signal(
            barrier, inc=1, device_id={"tile": lax.rem(me + k, tiles)}, device_id_type=pl.DeviceIdType.MESH
        )
        return carry

    lax.fori_loop(1, tiles, greet, 0)
    own_r = pltpu.make_async_copy(res, rn.at[:, pl.ds(MARGIN, planes)], loc_sem.at[0])
    own_c = pltpu.make_async_copy(coup, cn.at[pl.ds(MARGIN, planes)], loc_sem.at[1])
    own_r.start()
    own_c.start()
    small = [
        pltpu.make_async_copy(src, dst, loc_sem.at[2 + i])
        for i, (src, dst) in enumerate(
            ((owners_in, owners), (earth_in, earth), (sweeps_in, sweeps), (inv_in, inv), (scale_in, scale))
        )
    ]
    for copy in small:
        copy.start()

    @pl.when(me == 0)
    def _():
        rn[:, :MARGIN] = jnp.zeros_like(rn[:, :MARGIN])
        cn[:MARGIN] = jnp.zeros_like(cn[:MARGIN])
        hl[...] = jnp.zeros_like(hl)

    @pl.when(me == last)
    def _():
        rn[:, ext - MARGIN :] = jnp.zeros_like(rn[:, ext - MARGIN :])
        cn[ext - MARGIN :] = jnp.zeros_like(cn[ext - MARGIN :])
        ys[:, planes] = jnp.zeros_like(ys[:, planes])

    def remote(src, dst, send, recv, peer):
        return pltpu.make_async_remote_copy(
            src_ref=src, dst_ref=dst, send_sem=send, recv_sem=recv,
            device_id={"tile": peer}, device_id_type=pl.DeviceIdType.MESH,
        )

    left, right = lax.rem(me + tiles - 1, tiles), lax.rem(me + 1, tiles)
    near_right, far_right, near_left, far_left = [], [], [], []
    for d in range(MARGIN):
        there, mirror = MARGIN - 1 - d, ext - MARGIN + d
        for copies, peer, here, lands in (
            (near_right if d == 0 else far_right, right, planes - 1 - d, there),
            (near_left if d == 0 else far_left, left, d, mirror),
        ):
            slot = 4 * d + (0 if peer is right else 2)
            copies.append(
                remote(res.at[:, here], rn.at[:, lands], halo_send.at[slot], halo_recv.at[slot], peer)
            )
            copies.append(
                remote(coup.at[here], cn.at[lands], halo_send.at[slot + 1], halo_recv.at[slot + 1], peer)
            )
    to_right, to_left = near_right + far_right, near_left + far_left

    def start(rightward, leftward):
        @pl.when(me < last)
        def _():
            for copy in rightward:
                copy.start()

        @pl.when(me > 0)
        def _():
            for copy in leftward:
                copy.start()

    xs[:, ext] = jnp.zeros_like(xs[:, ext])
    hs[:, 0] = jnp.zeros_like(hs[:, 0])

    def prepare(p):
        c = cn[p]
        q = damping / (16.0 + c * c)
        a, b = 4.0 * q, c * q
        coef[0, p], coef[1, p], coef[2, p] = a, b, c
        for k in range(3):
            real, imag = rn[k, p], rn[k + 3, p]
            xs[k, p] = a * real + b * imag
            xs[k + 3, p] = a * imag - b * real

    for copy in small:
        copy.wait()

    cells = 6 * ny
    col = iota((8, cells), 1)
    row_in = lax.rem(col, ny)
    y_of = row_in
    chan = col // ny
    parity = lax.rem(y_of // 4, 2)
    keys = []
    for zb in range(zblocks):
        key = jnp.full((8, cells), -1, jnp.int32)
        for yb in range(ny // 8):
            b = yb * zblocks + zb
            value = jnp.where(earth[0, b] == 1, owners[0, b], -1)
            key = jnp.where(y_of // 8 == yb, value, key)
        keys.append(key)
    mine = chan == iota((8, cells), 0)
    combos = [(par, zb) for par in range(2) for zb in range(zblocks)]

    def spread(par, zb, flip, weight, lanes):
        z, lane = iota((nz, lanes), 0), iota((nz, lanes), 1)
        if flip:
            z, lane = iota((lanes, nz), 1), iota((lanes, nz), 0)
        lane = lax.rem(lane, 32) if one_phase else lane
        hit = (z // 64 == zb) & (lane == par * 16 + lax.rem(z, 64) // 4)
        return jnp.where(hit, weight, 0.0).astype(F32)

    def mark(group, carry):
        for j, (par, zb) in enumerate(combos):
            for o in range(8):
                hit = mine & (parity == par) & (keys[zb] == group * 8 + o)
                w_ref[group, j * 64 + o * 8 : j * 64 + o * 8 + 8] = jnp.where(hit, 1.0, 0.0).astype(F32)
        return carry

    if one_phase:
        mark(0, 0)
    else:
        lax.fori_loop(0, tiles // 8, mark, 0)
    own_r.wait()
    own_c.wait()
    pl.semaphore_wait(barrier, tiles - 1)
    start(near_right, near_left)

    sums = []
    for k in range(6):
        total = rn[k, MARGIN]
        for p in range(MARGIN + 1, MARGIN + planes):
            total = total + rn[k, p]
        sums.append(total)
    sums = jnp.concatenate(sums, axis=0)
    wide = inbox.shape[2]

    def dot(x, y):
        return jnp.dot(x, y, precision=HIGH, preferred_element_type=F32)

    def restrict(group, carry):
        partial = dot(w_ref[group], sums)
        agg = jnp.zeros((64, wide), F32)
        for j, (par, zb) in enumerate(combos):
            agg = agg + dot(partial[j * 64 : j * 64 + 64], spread(par, zb, False, 1.0 / 64.0, wide))
        if one_phase:
            outbox[0] = dot(gather_rows, jnp.where(own_slot, agg, 0.0))
        else:
            for o in range(8):
                outbox[group * 8 + o] = agg[o * 8 : o * 8 + 8]
        return carry

    own_slot = lax.rem(iota((64, wide), 0), 8) == iota((64, wide), 1) // 32
    gather_rows = jnp.where(iota((8, 64), 0) == iota((8, 64), 1) // 8, 1.0, 0.0).astype(F32)
    if one_phase:
        restrict(0, 0)
    else:
        lax.fori_loop(0, tiles // 8, restrict, 0)

    def sum_copy(k, source):
        peer = lax.rem(me + k, tiles)
        slot = peer if source else me
        box = outbox.at[0] if one_phase else outbox.at[peer]
        return remote(box, inbox.at[slot], s1.at[k], r1.at[slot], peer)

    def scale_copy(k, source):
        peer = lax.rem(me + k, tiles)
        slot = peer if source else me
        return remote(scale_in, sbox.at[slot], s2.at[k], r2.at[slot], peer)

    def send_sum(k, carry):
        sum_copy(k, False).start()
        if one_phase:
            scale_copy(k, False).start()
        return carry

    lax.fori_loop(1, tiles, send_sum, 0)
    start(far_right, far_left)
    if one_phase:
        inbox[me] = outbox[0]
        sbox[me] = scale[...]
    else:
        inbox[me] = outbox[me]

    for p in range(MARGIN, MARGIN + planes):
        prepare(p)

    def wait_sum(k, carry):
        copies = [sum_copy(k, True)] + ([scale_copy(k, True)] if one_phase else [])
        for done in copies:
            done.wait_send()
            done.wait_recv()
        return carry

    def prolong(group, carry):
        if one_phase:
            total = inbox[0]
            for t in range(1, tiles):
                total = total + inbox[t]
            width = inv.shape[0]
            corr = lax.dot_general(
                total[:, :width], inv[...], (((1,), (1,)), ((), ())), precision=HIGH, preferred_element_type=F32
            )
            corr = corr * jnp.concatenate([sbox[t] for t in range(tiles)], axis=0)
            rows, lanes = iota((64, width), 0), iota((64, width), 1)
            copy_rows = jnp.where(iota((64, 8), 0) // 8 == iota((64, 8), 1), 1.0, 0.0).astype(F32)
            box = jnp.where(lax.rem(rows, 8) == lanes // 32, dot(copy_rows, corr), 0.0)
        else:
            width = 128
            box = jnp.concatenate([cbox[group * 8 + o] for o in range(8)], axis=0)
        parts = [dot(box, spread(par, zb, True, 1.0, width)) for par, zb in combos]
        value = lax.dot_general(
            w_ref[group], jnp.concatenate(parts, axis=0), (((0,), (0,)), ((), ())),
            precision=HIGH, preferred_element_type=F32,
        )
        fine[...] = value if one_phase else fine[...] + value
        return carry

    if one_phase:
        lax.fori_loop(1, tiles, wait_sum, 0)
        prolong(0, 0)

    @pl.when(me > 0)
    def _():
        for copy in to_right:
            copy.wait_recv()

    for p in range(MARGIN):
        prepare(p)

    @pl.when(me < last)
    def _():
        for copy in to_left:
            copy.wait_recv()

    for p in range(ext - MARGIN, ext):
        prepare(p)

    def faces(src, p, f, ahead=True):
        ex, ey, ez = src[f, p], src[f + 1, p], src[f + 2, p]
        ney, nez = -ey, ez
        if ahead:
            ney, nez = src[f + 1, p + 1] - ey, ez - src[f + 2, p + 1]
        hx = (y_next(ez) - ez) - (z_next(ey) - ey)
        hy = (z_next(ex) - ex) + nez
        hz = ney - (y_next(ex) - ex)
        return hx, hy, hz

    def edge(src, p, f, k):
        if k == 0:
            hy, hz = src[f + 1, p + 1], src[f + 2, p + 1]
            return (hz - y_prev(hz)) - (hy - z_prev(hy))
        hx = src[f, p + 1]
        if k == 1:
            return (hx - z_prev(hx)) - (src[f + 2, p + 1] - src[f + 2, p])
        return (src[f + 1, p + 1] - src[f + 1, p]) - (hx - y_prev(hx))

    def all_faces(first, stop):
        for p in range(first, stop):
            for f in (0, 3):
                hs[f, p + 1], hs[f + 1, p + 1], hs[f + 2, p + 1] = faces(xs, p, f)

    count = sweeps[0, 0]

    def update(p, active, store):
        c = coef[2, p]
        a, b = coef[0, p] * active, coef[1, p] * active
        for k in range(3):
            u, w = xs[k, p], xs[k + 3, p]
            real = rn[k, p] - edge(hs, p, 0, k) + c * w
            imag = rn[k + 3, p] - edge(hs, p, 3, k) - c * u
            store(k, p, u + (a * real + b * imag))
            store(k + 3, p, w + (a * imag - b * real))

    def keep(k, p, value):
        xs[k, p] = value

    def sweep(step, first, stop):
        active = jnp.where(step < count, 1.0, 0.0).astype(F32)
        all_faces(max(first - 1, 0), stop)
        for p in range(first, stop):
            update(p, active, keep)

    def full(step, carry):
        sweep(step, 0, ext)
        return carry

    cut = SWEEPS // 2
    lax.fori_loop(1, cut, full, 0)
    if not one_phase:
        lax.fori_loop(1, tiles, wait_sum, 0)
        total = lax.fori_loop(0, tiles, lambda t, acc: acc + inbox[t], jnp.zeros((8, 128), F32))
        width = inv.shape[0]
        fold = jnp.where(iota((128, width), 0) == lax.rem(iota((128, width), 1), 32), 1.0, 0.0).astype(F32)
        unfold = jnp.where(iota((width, 128), 1) == lax.rem(iota((width, 128), 0), 32), 1.0, 0.0).astype(F32)
        own_channel = iota((8, width), 0) == iota((8, width), 1) // 32
        flat = jnp.where(own_channel, jnp.dot(total, fold, precision=HIGH, preferred_element_type=F32), 0.0)
        flat = jnp.broadcast_to(jnp.sum(flat, axis=0, keepdims=True), (8, width))
        corr = lax.dot_general(flat, inv[...], (((1,), (1,)), ((), ())), precision=HIGH, preferred_element_type=F32)
        corr = jnp.where(own_channel, corr * scale[...], 0.0)
        csrc[...] = jnp.dot(corr, unfold, precision=HIGH, preferred_element_type=F32)

        def send_corr(k, carry):
            peer = lax.rem(me + k, tiles)
            remote(csrc, cbox.at[me], s2.at[k], r2.at[me], peer).start()
            return carry

        lax.fori_loop(1, tiles, send_corr, 0)
        cbox[me] = csrc[...]

    lax.fori_loop(cut, SWEEPS - 2, full, 0)
    sweep(SWEEPS - 2, MARGIN - 1, MARGIN + planes + 1)

    if not one_phase:

        def wait_corr(k, carry):
            peer = lax.rem(me + k, tiles)
            done = remote(csrc, cbox.at[peer], s2.at[k], r2.at[peer], peer)
            done.wait_send()
            done.wait_recv()
            return carry

        lax.fori_loop(1, tiles, wait_corr, 0)
        fine[...] = jnp.zeros_like(fine)

        lax.fori_loop(0, tiles // 8, prolong, 0)

    active = jnp.where(SWEEPS - 1 < count, 1.0, 0.0).astype(F32)
    all_faces(MARGIN + planes - 2, MARGIN + planes)

    def finish(k, p, value):
        value = value + fine[k * ny : k * ny + ny]
        ys[k, p - MARGIN] = value
        pre[k, p - MARGIN] = value

    update(MARGIN + planes - 1, active, finish)
    for i, f in enumerate((0, 3)):
        hx, hy, hz = faces(ys, planes - 1, f, ahead=False)
        gx[i], gs[2 * i], gs[2 * i + 1] = hx, hy, hz
    exit_right = [remote(gs, hl, fs.at[0], fr.at[0], right)]

    @pl.when(me < last)
    def _():
        for copy in exit_right:
            copy.start()

    all_faces(MARGIN - 1, MARGIN + planes - 2)
    update(MARGIN, active, finish)
    exit_left = [
        remote(ys.at[lo:hi, 0], ys.at[lo:hi, planes], fs.at[1 + i], fr.at[1 + i], left)
        for i, (lo, hi) in enumerate(SPLIT)
    ]

    @pl.when(me > 0)
    def _():
        for copy in exit_left:
            copy.start()

    for p in range(MARGIN + 1, MARGIN + planes - 1):
        update(p, active, finish)
    for p in range(planes - 1):
        for f in (0, 3):
            hs[f, p + 1], hs[f + 1, p + 1], hs[f + 2, p + 1] = faces(ys, p, f)

    def image(p):
        c = coef[2, p + MARGIN]
        for k in range(3):
            img[k, p] = edge(hs, p, 0, k) - c * ys[k + 3, p]
            img[k + 3, p] = edge(hs, p, 3, k) + c * ys[k, p]

    for p in range(1, planes - 1):
        image(p)

    @pl.when(me > 0)
    def _():
        for copy in exit_right:
            copy.wait_recv()

    leading = jnp.where(me > 0, 1.0, 0.0).astype(F32)
    for i, f in enumerate((0, 3)):
        hs[f + 1, 0] = (hl[2 * i] - ys[f + 2, 0]) * leading
        hs[f + 2, 0] = (hl[2 * i + 1] + ys[f + 1, 0]) * leading
    image(0)

    @pl.when(me < last)
    def _():
        for copy in exit_left:
            copy.wait_recv()

    for i, f in enumerate((0, 3)):
        hs[f, planes] = gx[i]
        hs[f + 1, planes] = gs[2 * i] - ys[f + 2, planes]
        hs[f + 2, planes] = gs[2 * i + 1] + ys[f + 1, planes]
    image(planes - 1)

    @pl.when(me < last)
    def _():
        for copy in to_right + exit_right:
            copy.wait_send()

    @pl.when(me > 0)
    def _():
        for copy in to_left + exit_left:
            copy.wait_send()


def store(pre, img, pre_out, img_out, sem):
    copies = [pltpu.make_async_copy(pre, pre_out, sem.at[0]), pltpu.make_async_copy(img, img_out, sem.at[1])]
    for copy in copies:
        copy.start()
    for copy in copies:
        copy.wait()


def shards(residual, coupling, owners, earth, sweep_counts, coarse_inverse, coarse_scale):
    tiles = lax.axis_size("tile")
    chans, planes, ny, nz = residual.shape
    ext = planes + 2 * MARGIN
    groups = -(-tiles // 8)
    wide = 2 * (nz // 64) * 64

    def field(*lead):
        return pltpu.VMEM((*lead, ny, nz), F32)

    hbm = pl.BlockSpec(memory_space=pltpu.HBM)
    vmem = pl.BlockSpec(memory_space=pltpu.VMEM)
    dma = pltpu.SemaphoreType.DMA
    grant = 67043328 - 2 * residual.size * 4 - 64 * 1024
    sweep_counts = sweep_counts.reshape(1, 1)
    staged = pltpu.VMEM(residual.shape, F32)
    shape = jax.ShapeDtypeStruct(residual.shape, F32)
    outs = pl.pallas_call(
        functools.partial(kernel, tiles),
        out_shape=(staged, staged),
        in_specs=[hbm] * 7,
        out_specs=(vmem, vmem),
        scratch_shapes=[
            pltpu.SMEM(owners.shape, jnp.int32),
            pltpu.SMEM(earth.shape, jnp.int32),
            pltpu.SMEM(sweep_counts.shape, jnp.int32),
            pltpu.VMEM(coarse_inverse.shape, F32),
            pltpu.VMEM(coarse_scale.shape, F32),
            field(chans, ext),
            field(ext),
            field(3, ext),
            field(chans, ext + 1),
            field(chans, ext + 1),
            field(chans, planes + 1),
            field(4),
            field(2),
            field(4),
            pltpu.VMEM((chans * ny, nz), F32),
            pltpu.VMEM((groups, wide, chans * ny), F32),
            pltpu.VMEM((groups * 8, 8, 256 if tiles == 8 else 128), F32),
            pltpu.VMEM((groups * 8, 8, 256 if tiles == 8 else 128), F32),
            pltpu.VMEM((groups * 8, 8, 128), F32),
            pltpu.VMEM((8, 128), F32),
            pltpu.VMEM((tiles, *coarse_scale.shape), F32),
            dma((7,)), dma((8,)), dma((8,)),
            dma((tiles,)), dma((tiles,)), dma((tiles,)), dma((tiles,)),
            dma((3,)), dma((3,)),
        ],
        compiler_params=pltpu.CompilerParams(
            collective_id=0, has_side_effects=True, vmem_limit_bytes=grant
        ),
        name="schwarz",
    )(residual, coupling, owners, earth, sweep_counts, coarse_inverse, coarse_scale)
    return pl.pallas_call(
        store,
        out_shape=(shape, shape),
        in_specs=[vmem, vmem],
        out_specs=(hbm, hbm),
        scratch_shapes=[dma((2,))],
        compiler_params=pltpu.CompilerParams(vmem_limit_bytes=1024 * 1024),
        name="store",
    )(*outs)


def solution(mesh):
    return jax.shard_map(
        shards,
        mesh=mesh,
        in_specs=(
            P("pair", "tile", None, None),
            P("tile", "pair", None),
            P("tile", None),
            P("tile", None),
            P("tile"),
            P("pair", None),
            P("tile", "pair"),
        ),
        out_specs=(P("pair", "tile", None, None), P("pair", "tile", None, None)),
        check_vma=False,
    )
```
